32 devices in a mesh: genome: 4 (over z), trow: 2 (over core), tcol: 4 (over y, x).
Axes of the slice: x: 2, y: 2, z: 4, core: 2. Of those that a mesh axis runs over, the one named last changes fastest.
Arguments:
- ldscore: float32 [4096], P('genome'), may hold values from 1 to 100
- zscores: bfloat16 [4096, 4096], P('genome', ('trow', 'tcol')), may hold values from -30 to 30
Outputs:
- rg: float32 [2, 2048, 2, 2048], P('trow', 'genome', None, 'tcol')
- rg_se: float32 [2, 2048, 2, 2048], P('trow', 'genome', None, 'tcol')
The draws below stay inside these ranges and needn't reach their ends.
All inputs are finite; a program needn't handle non-finite values.
Results may differ from the reference program's by a relative error of at most 0.038.
Values may be sent and summed in bfloat16 or wider, within the bound.
No kernel may reach another device: no remote copies, remote signals or barrier semaphores. Data moves between devices by JAX's collectives and lax.ppermute only.
A program may use at most 192 MiB of HBM per device.

```python
import math
import jax
import jax.numpy as jnp
from jax import lax

TRAITS = 4096
S_DEV = 1024
SNPS = 4096
N_GENOME = 4
N_TROW = 2


def ld_table(key):
    block_count = SNPS // S_DEV
    centre = jax.random.uniform(jax.random.fold_in(key, 21), (block_count,), jnp.float32, math.log(1.2), math.log(60.0))
    within = jax.random.uniform(jax.random.fold_in(key, 11), (block_count, S_DEV), jnp.float32, -0.7, 0.7)
    raw = (centre[:, None] + within).reshape(SNPS)
    return jnp.clip(jnp.exp(raw), 1.0, 100.0)


def draw_ldscore(key, part):
    return ld_table(key)


def draw_zscores(key, part):
    ld_vals = ld_table(key)
    top_herit = 0.05
    herit = jnp.exp(jax.random.uniform(jax.random.fold_in(key, 12), (TRAITS,), jnp.float32, math.log(0.0008), math.log(top_herit)))
    group = jax.random.randint(jax.random.fold_in(key, 13), (TRAITS,), 0, 8)
    noise_group = jax.random.randint(jax.random.fold_in(key, 18), (TRAITS,), 0, 8)
    share = jax.random.uniform(jax.random.fold_in(key, 14), (TRAITS,), jnp.float32, 0.3, 0.95)
    common = jax.random.normal(jax.random.fold_in(key, 15), (SNPS, 8), jnp.float32)
    private = jax.random.normal(jax.random.fold_in(key, 16), (SNPS, TRAITS), jnp.float32)
    own_noise = jax.random.normal(jax.random.fold_in(key, 17), (SNPS, TRAITS), jnp.float32)
    shared_noise = jax.random.normal(jax.random.fold_in(key, 19), (SNPS, 8), jnp.float32)
    picked = jnp.take(common, group, axis=1)
    genetic = share[None, :] * picked + jnp.sqrt(1.0 - share * share)[None, :] * private
    noise = math.sqrt(0.85) * own_noise + math.sqrt(0.15) * jnp.take(shared_noise, noise_group, axis=1)
    zvalue = noise + jnp.sqrt(herit[None, :] * ld_vals[:, None]) * genetic
    return jnp.clip(zvalue, -30.0, 30.0).astype(jnp.bfloat16)


def setup_inputs(seed: int = 0) -> dict:
    seeds = jax.random.split(jax.random.key(seed), 3)
    ldscore = draw_ldscore(jax.random.fold_in(seeds[2], 71), 0)
    zscores = draw_zscores(jax.random.fold_in(seeds[2], 71), 0)
    return {"ldscore": ldscore, "zscores": zscores}


floor_value = 0.002

def slope_fit(inv_sum, ld_sum, y_sum, l_sum, count):
    return (inv_sum * l_sum - count * y_sum) / (inv_sum * ld_sum - count * count)

def weights_for(herit_pos, ld_column):
    return (1.0 / (1.0 + herit_pos[None, :] * ld_column[:, None])).astype(jnp.bfloat16)

def coupling(tiles):
    return (tiles[2] * tiles[1] - tiles[3] * tiles[0]) / (tiles[2] * tiles[4] - tiles[3] * tiles[3])

def reference(ldscore, zscores):
    blocks = N_GENOME
    ld_weight = 1.0 / ldscore
    z_float = zscores.astype(jnp.float32)
    z_square = z_float * z_float
    stat_y = lax.optimization_barrier(jnp.sum((z_square * ld_weight[:, None]).reshape(blocks, S_DEV, TRAITS), axis=1))
    stat_l = lax.optimization_barrier(jnp.sum(z_square.reshape(blocks, S_DEV, TRAITS), axis=1))
    stat_inv = lax.optimization_barrier(jnp.sum(ld_weight.reshape(blocks, S_DEV), axis=1))
    stat_ld = lax.optimization_barrier(jnp.sum(ldscore.reshape(blocks, S_DEV), axis=1))
    total_inv = jnp.sum(stat_inv)
    total_ld = jnp.sum(stat_ld)
    total_y = lax.optimization_barrier(jnp.sum(stat_y, axis=0))
    total_l = lax.optimization_barrier(jnp.sum(stat_l, axis=0))
    herit_full = slope_fit(total_inv, total_ld, total_y, total_l, float(S_DEV * blocks))
    herit_del = slope_fit((total_inv - stat_inv)[:, None], (total_ld - stat_ld)[:, None], total_y[None] - stat_y, total_l[None] - stat_l, float(S_DEV * (blocks - 1)))
    herit_pos = jnp.maximum(herit_full, 0.0)
    weight_u = weights_for(herit_pos, ldscore)
    u_float = weight_u.astype(jnp.float32)
    scaled = z_float * u_float
    weighted_z = scaled.astype(jnp.bfloat16)
    weighted_zinv = (scaled * ld_weight[:, None]).astype(jnp.bfloat16)
    weight_inv = (u_float * ld_weight[:, None]).astype(jnp.bfloat16)
    weight_ld = (u_float * ldscore[:, None]).astype(jnp.bfloat16)
    rows_all = jnp.stack([weighted_zinv, weighted_z, weight_inv, weight_u, weight_ld])
    z_cols = weighted_z.astype(jnp.float32).reshape(blocks, S_DEV, TRAITS)
    u_cols = u_float.reshape(blocks, S_DEV, TRAITS)
    herit_floor = jnp.maximum(herit_full, floor_value)
    del_floor = jnp.maximum(herit_del, floor_value)
    row_block = min(256, TRAITS)

    def one_block(start):
        rows = lax.dynamic_slice_in_dim(rows_all, start, row_block, axis=2).astype(jnp.float32)
        rows = rows.reshape(5, blocks, S_DEV, row_block)
        sums = jnp.stack([jnp.einsum('gsi,gsj->gij', rows[0], z_cols), jnp.einsum('gsi,gsj->gij', rows[1], z_cols), jnp.einsum('gsi,gsj->gij', rows[2], u_cols), jnp.einsum('gsi,gsj->gij', rows[3], u_cols), jnp.einsum('gsi,gsj->gij', rows[4], u_cols)])
        tiles = lax.optimization_barrier(sums.astype(jnp.bfloat16)).astype(jnp.float32)
        totals = lax.optimization_barrier(jnp.sum(tiles, axis=1))
        deleted = totals[:, None] - tiles
        full_g = coupling(totals)
        del_g = coupling(deleted)
        rows_full = lax.dynamic_slice_in_dim(herit_floor, start, row_block)
        rows_del = lax.dynamic_slice_in_dim(del_floor, start, row_block, axis=1)
        rg_rows = full_g / jnp.sqrt(rows_full[:, None] * herit_floor[None, :])
        rg_del = del_g / jnp.sqrt(rows_del[:, :, None] * del_floor[:, None, :])
        mean_del = lax.optimization_barrier(jnp.mean(rg_del, axis=0))
        diff = rg_del - mean_del[None]
        spread = lax.optimization_barrier(jnp.sum(diff * diff, axis=0))
        se_rows = jnp.sqrt((blocks - 1) / blocks * spread)
        return (rg_rows, se_rows)
    starts = (jnp.arange(TRAITS // row_block) * row_block).astype(jnp.int32)
    rg_blocks, se_blocks = lax.map(one_block, starts)
    shape = (N_TROW, TRAITS // N_TROW, N_TROW, TRAITS // N_TROW)
    return (rg_blocks.reshape(shape), se_blocks.reshape(shape))
```

```python
import functools

import jax
import jax.numpy as jnp
from jax import lax
from jax.experimental import pallas as pl
from jax.experimental.pallas import tpu as pltpu
from jax.sharding import PartitionSpec as P

floor_value = 0.002
axes = ("genome", "trow", "tcol")
bf16 = jnp.bfloat16
f32 = jnp.float32
lanes = 128
vmem_bytes = 56 << 20


def contract(left, right):
    return lax.dot_general(
        left, right, (((0,), (0,)), ((), ())), preferred_element_type=f32
    )


def slope_fit(inv_sum, ld_sum, y_sum, l_sum, count):
    return (inv_sum * l_sum - count * y_sum) / (inv_sum * ld_sum - count * count)


def weights_for(herit_pos, ld_column):
    return (1.0 / (1.0 + herit_pos[None, :] * ld_column[:, None])).astype(bf16)


def coupling(tiles):
    return (tiles[2] * tiles[1] - tiles[3] * tiles[0]) / (tiles[2] * tiles[4] - tiles[3] * tiles[3])


def split_rows(value):
    high = value.astype(bf16).astype(f32)
    rest = value - high
    middle = rest.astype(bf16).astype(f32)
    return [high, middle, rest - middle]


def down_sublanes(row):
    return jnp.transpose(jnp.broadcast_to(row, (lanes, lanes)))


def widen(column, width):
    return jnp.concatenate([column] * (width // lanes), axis=1)


def message_kernel(parts, idx, z_ref, ld_ref, ldrow_ref, *outs):
    snps, width = z_ref.shape
    piece = snps // parts
    y_acc = jnp.zeros((8, width), f32)
    l_acc = jnp.zeros((8, width), f32)
    for chunk in range(snps // lanes):
        weight = widen(down_sublanes(1.0 / ld_ref[chunk : chunk + 1, :]), width)
        values = z_ref[chunk * lanes : (chunk + 1) * lanes, :].astype(f32)
        square = values * values
        l_acc = l_acc + jnp.sum(square.reshape(lanes // 8, 8, width), axis=0)
        y_acc = y_acc + jnp.sum((square * weight).reshape(lanes // 8, 8, width), axis=0)
    rows = split_rows(jnp.sum(y_acc, axis=0, keepdims=True))
    rows = rows + split_rows(jnp.sum(l_acc, axis=0, keepdims=True))
    rows = rows + split_rows(ldrow_ref[...])
    tail = outs[0].shape[0] - piece
    used = sum(row.shape[0] for row in rows)
    rows = rows + [jnp.zeros((tail - used, width), f32)]
    extra = jnp.concatenate(rows, axis=0).astype(bf16)
    column = idx[2]
    for step, out in enumerate(outs):
        quarter = jnp.bitwise_xor(column, step)
        out[:piece, :] = z_ref[pl.ds(pl.multiple_of(quarter * piece, piece), piece), :]
        out[piece:, :] = extra


def route_kernel(parts, idx, *refs):
    ins, outs = refs[:parts], refs[parts:]
    for shift in range(parts):
        chosen = jnp.bitwise_xor(idx[2], lax.rem(idx[0] + shift, parts))
        for step in range(parts):

            @pl.when(chosen == step)
            def _(shift=shift, step=step):
                outs[shift][...] = ins[step][...]


def join_kernel(parts, idx, *refs):
    ins, (rows_ref, stat_ref, ld_ref) = refs[:parts], refs[parts:]
    piece, width = rows_ref.shape[1:]
    ld_rows = ld_ref.shape[0] // parts
    for shift in range(parts):
        block = lax.rem(idx[0] + parts - shift, parts)
        rows_ref[block] = ins[shift][:piece, :]
        extra = ins[shift][piece:, :].astype(f32)
        stat_ref[pl.ds(block, 1), :] = (extra[2:3] + extra[1:2]) + extra[0:1]
        stat_ref[pl.ds(parts + block, 1), :] = (extra[5:6] + extra[4:5]) + extra[3:4]
        for row in range(ld_rows):
            at = 6 + row
            ld_ref[pl.ds(block * ld_rows + row, 1), :] = (
                extra[at + 2 * ld_rows : at + 2 * ld_rows + 1]
                + extra[at + ld_rows : at + ld_rows + 1]
            ) + extra[at : at + 1]


def total(values):
    return jnp.sum(jnp.sum(values, axis=1, keepdims=True), axis=0, keepdims=True)


def herit_full(stats, ld, blocks, snps):
    inv = total(1.0 / ld)
    return slope_fit(
        inv,
        total(ld),
        jnp.sum(stats[:blocks], axis=0, keepdims=True),
        jnp.sum(stats[blocks:], axis=0, keepdims=True),
        float(snps * blocks),
    )


def herit_without(stats, ld, block, blocks, snps):
    per = ld.shape[0] // blocks
    inv = [total(1.0 / ld[b * per : (b + 1) * per]) for b in range(blocks)]
    lds = [total(ld[b * per : (b + 1) * per]) for b in range(blocks)]
    y_total = jnp.sum(stats[:blocks], axis=0, keepdims=True)
    l_total = jnp.sum(stats[blocks:], axis=0, keepdims=True)
    inv_total, ld_total = sum(inv[1:], inv[0]), sum(lds[1:], lds[0])
    return slope_fit(
        inv_total - inv[block],
        ld_total - lds[block],
        y_total - stats[block : block + 1],
        l_total - stats[blocks + block : blocks + block + 1],
        float(snps * (blocks - 1)),
    )


def weight_kernel(
    blocks, idx, row_stat, own_stat, mate_stat, ld_ref, sums_ref, urow_ref, ucol_ref, ldcol_ref, inv_ref, wld_ref
):
    snps, width = urow_ref.shape
    block = pl.program_id(0)
    ld = ld_ref[...]
    side = idx[1]
    here = [pl.multiple_of(side * width, width), pl.multiple_of((1 - side) * width, width)]
    herit_row = jnp.maximum(herit_full(row_stat[...], ld, blocks, snps), 0.0)
    herit_col = [
        jnp.maximum(herit_full(stat[...], ld, blocks, snps), 0.0) for stat in (own_stat, mate_stat)
    ]
    per = snps // width
    step = width // lanes
    row_of = lax.broadcasted_iota(jnp.int32, ld.shape, 0)
    here_ld = [
        jnp.sum(jnp.where(row_of == block * per + k, ld, 0.0), axis=0, keepdims=True) for k in range(per)
    ]
    for chunk in range(snps // lanes):
        at = slice(chunk * lanes, (chunk + 1) * lanes)
        column = down_sublanes(here_ld[chunk // step][:, (chunk % step) * lanes : (chunk % step + 1) * lanes])
        ldcol_ref[at, :] = column
        ld_wide = widen(column, width)
        inv_wide = 1.0 / column
        inv_wide = widen(inv_wide, width)
        u_row = (1.0 / (1.0 + herit_row * ld_wide)).astype(bf16)
        urow_ref[at, :] = u_row
        u_float = u_row.astype(f32)
        inv_ref[at, :] = (u_float * inv_wide).astype(bf16)
        wld_ref[at, :] = (u_float * ld_wide).astype(bf16)
        for half in range(2):
            ucol_ref[at, pl.ds(here[half], width)] = (
                1.0 / (1.0 + herit_col[half] * ld_wide)
            ).astype(bf16)
    u_col = ucol_ref[...]
    sums_ref[0] = contract(inv_ref[...], u_col).astype(bf16)
    sums_ref[1] = contract(urow_ref[...], u_col).astype(bf16)
    sums_ref[2] = contract(wld_ref[...], u_col).astype(bf16)


def pair_kernel(parts, idx, *refs):
    pieces = refs[:parts]
    own_ref, mate_ref, urow_ref, ucol_ref, ldcol_ref, out_ref, zu_ref, zinv_ref, zcol_ref = refs[parts:]
    piece, width = pieces[0].shape
    side = idx[1]
    for half, ref in enumerate((own_ref, mate_ref)):
        place = side if half == 0 else 1 - side
        at = pl.ds(pl.multiple_of(place * width, width), width)
        zcol_ref[:, at] = (ref[...].astype(f32) * ucol_ref[:, at].astype(f32)).astype(bf16)
    for step in range(parts):
        start = pl.multiple_of(jnp.bitwise_xor(idx[2], step) * piece, piece)
        at = pl.ds(start, piece)
        scaled = pieces[step][...].astype(f32) * urow_ref[at, :].astype(f32)
        zu_ref[at, :] = scaled.astype(bf16)
        zinv_ref[at, :] = (scaled * widen(1.0 / ldcol_ref[at, :], width)).astype(bf16)
    z_col = zcol_ref[...]
    out_ref[0] = contract(zinv_ref[...], z_col).astype(bf16)
    out_ref[1] = contract(zu_ref[...], z_col).astype(bf16)


def finish_kernel(blocks, snps, idx, row_stat, own_stat, mate_stat, ld_ref, w_ref, *refs):
    pairs, (rg_ref, se_ref) = refs[:blocks], refs[blocks:]
    tile = rg_ref.shape[1]
    width = rg_ref.shape[3]
    ld = ld_ref[...]
    side = idx[1]
    start = pl.multiple_of(pl.program_id(0) * tile, tile)

    def scale(value):
        return lax.rsqrt(jnp.maximum(value, floor_value))

    def all_scales(ref):
        stats = ref[...]
        scales = [scale(herit_full(stats, ld, blocks, snps))]
        return scales + [scale(herit_without(stats, ld, b, blocks, snps)) for b in range(blocks)]

    row_scales = [down_sublanes(value) for value in all_scales_rows(row_stat, start, tile, ld, blocks, snps, scale)]
    own, mate = all_scales(own_stat), all_scales(mate_stat)
    for half in range(2):
        col_scales = [jnp.where(side == half, a, b) for a, b in zip(own, mate)]
        at = slice(half * width, (half + 1) * width)
        y0 = [pairs[s][0, :, at].astype(f32) for s in range(blocks)]
        y1 = [pairs[s][1, :, at].astype(f32) for s in range(blocks)]
        block_of = [idx[3 + s] for s in range(blocks)]
        w = [[w_ref[block_of[s], k, :, at].astype(f32) for s in range(blocks)] for k in range(3)]
        tiles = [y0, y1] + w
        sums = [sum(t[1:], t[0]) for t in tiles]
        rg_ref[0, :, half, :] = coupling(sums) * (widen(row_scales[0], width) * col_scales[0])
        dels = []
        for s in range(blocks):
            row_scale, col_scale = row_scales[1], col_scales[1]
            for b in range(1, blocks):
                row_scale = jnp.where(block_of[s] == b, row_scales[1 + b], row_scale)
                col_scale = jnp.where(block_of[s] == b, col_scales[1 + b], col_scale)
            rest = [total_ - t[s] for total_, t in zip(sums, tiles)]
            dels.append(coupling(rest) * (widen(row_scale, width) * col_scale))
        mean = sum(dels[1:], dels[0]) * (1.0 / blocks)
        spread = sum([(d - mean) * (d - mean) for d in dels[1:]], (dels[0] - mean) * (dels[0] - mean))
        se_ref[0, :, half, :] = jnp.sqrt((blocks - 1) / blocks * spread)


def all_scales_rows(ref, start, tile, ld, blocks, snps, scale):
    stats = ref[:, pl.ds(start, tile)]
    scales = [scale(herit_full(stats, ld, blocks, snps))]
    return scales + [scale(herit_without(stats, ld, b, blocks, snps)) for b in range(blocks)]


def whole(shape):
    return pl.BlockSpec(shape, lambda *_: (0,) * len(shape))


def call(kernel, idx, ins, in_specs, outs, out_specs, grid=(1,), scratch=()):
    return pl.pallas_call(
        kernel,
        grid_spec=pltpu.PrefetchScalarGridSpec(
            num_scalar_prefetch=1,
            grid=grid,
            in_specs=in_specs,
            out_specs=out_specs,
            scratch_shapes=list(scratch),
        ),
        out_shape=outs,
        compiler_params=pltpu.CompilerParams(vmem_limit_bytes=vmem_bytes),
    )(idx, *ins)


def square_device(sizes, ldscore, zscores):
    blocks, grid_rows, parts = sizes
    snps, width = zscores.shape
    piece = snps // parts
    g, r, c = (lax.axis_index(name) for name in axes)

    def move(value, target):
        pairs = []
        for gi in range(blocks):
            for ri in range(grid_rows):
                for ci in range(parts):
                    to = target(gi, ri, ci)
                    if to is not None:
                        source = (gi * grid_rows + ri) * parts + ci
                        pairs.append((source, (to[0] * grid_rows + to[1]) * parts + to[2]))
        return lax.ppermute(value, axes, pairs)

    def swap(value):
        return move(value, lambda gi, ri, ci: (gi, 1 - ri, ci))

    def line(value, table):
        return move(value, lambda gi, ri, ci: (table[gi], ri, ci) if gi in table else None)

    low = g < 2
    slot_blocks = [g, jnp.bitwise_xor(g, 1), jnp.where(low, 2, 1), jnp.where(low, 3, 0)]
    idx = jnp.stack([g, r, c] + slot_blocks).astype(jnp.int32)

    near = line(zscores, {0: 1, 1: 0, 2: 3, 3: 2})
    inner = line(zscores, {1: 2, 2: 1})

    ld_rows = snps // width
    extra = -(-(6 + 3 * ld_rows) // 16) * 16
    message = jax.ShapeDtypeStruct((piece + extra, width), bf16)
    sent = call(
        functools.partial(message_kernel, parts),
        idx,
        (zscores, ldscore.reshape(snps // lanes, lanes), ldscore.reshape(ld_rows, width)),
        [whole((snps, width)), whole((snps // lanes, lanes)), whole((ld_rows, width))],
        [message] * parts,
        [whole(message.shape)] * parts,
    )
    held = [sent[0]] + [
        move(sent[step], lambda gi, ri, ci, step=step: (gi, ri, ci ^ step)) for step in range(1, parts)
    ]
    routed = call(
        functools.partial(route_kernel, parts),
        idx,
        held,
        [whole(message.shape)] * parts,
        [message] * parts,
        [whole(message.shape)] * parts,
    )
    arrived = [routed[0]] + [
        line(routed[step], {gi: (gi + step) % blocks for gi in range(blocks)}) for step in range(1, blocks)
    ]
    quarter_rows, row_stat, ld_all = call(
        functools.partial(join_kernel, parts),
        idx,
        arrived,
        [whole(message.shape)] * parts,
        [
            jax.ShapeDtypeStruct((blocks, piece, width), bf16),
            jax.ShapeDtypeStruct((2 * blocks, width), f32),
            jax.ShapeDtypeStruct((blocks * ld_rows, width), f32),
        ],
        [whole((blocks, piece, width)), whole((2 * blocks, width)), whole((blocks * ld_rows, width))],
    )
    own_stat = move(row_stat, lambda gi, ri, ci: (ci, ri, gi))
    mate_stat = swap(own_stat)
    rows = [quarter_rows] + [
        move(quarter_rows, lambda gi, ri, ci, step=step: (gi, ri, ci ^ step)) for step in range(1, parts)
    ]

    outer = line(inner, {1: 0, 2: 3})
    cross = line(near, {1: 2, 2: 1})
    last = line(cross, {1: 0, 2: 3})
    own = [zscores, near, inner + outer, cross + last]
    mate = [swap(value) for value in own]

    stat_spec = whole((2 * blocks, width))
    ld_spec = whole((blocks * ld_rows, width))
    wide = grid_rows * width
    w_sums, u_row, u_col, ld_col = call(
        functools.partial(weight_kernel, blocks),
        idx,
        (row_stat, own_stat, mate_stat, ld_all),
        [stat_spec] * 3 + [ld_spec],
        [
            jax.ShapeDtypeStruct((blocks, 3, width, wide), bf16),
            jax.ShapeDtypeStruct((blocks, snps, width), bf16),
            jax.ShapeDtypeStruct((blocks, snps, wide), bf16),
            jax.ShapeDtypeStruct((blocks, snps, lanes), f32),
        ],
        [
            pl.BlockSpec((None, 3, width, wide), lambda b, _: (b, 0, 0, 0)),
            pl.BlockSpec((None, snps, width), lambda b, _: (b, 0, 0)),
            pl.BlockSpec((None, snps, wide), lambda b, _: (b, 0, 0)),
            pl.BlockSpec((None, snps, lanes), lambda b, _: (b, 0, 0)),
        ],
        grid=(blocks,),
        scratch=[pltpu.VMEM((snps, width), bf16)] * 2,
    )
    pairs = []
    for slot in range(blocks):
        pick = lambda i, ref, slot=slot: (ref[3 + slot], 0, 0)
        pairs.append(
            call(
                functools.partial(pair_kernel, parts),
                idx,
                (*rows, own[slot], mate[slot], u_row, u_col, ld_col),
                [pl.BlockSpec((None, piece, width), pick)] * parts
                + [whole((snps, width))] * 2
                + [
                    pl.BlockSpec((None, snps, width), pick),
                    pl.BlockSpec((None, snps, wide), pick),
                    pl.BlockSpec((None, snps, lanes), pick),
                ],
                jax.ShapeDtypeStruct((2, width, wide), bf16),
                whole((2, width, wide)),
                scratch=[
                    pltpu.VMEM((snps, width), bf16),
                    pltpu.VMEM((snps, width), bf16),
                    pltpu.VMEM((snps, wide), bf16),
                ],
            )
        )
    tile = lanes
    out = jax.ShapeDtypeStruct((1, width, grid_rows, width), f32)
    out_spec = pl.BlockSpec((1, tile, grid_rows, width), lambda i, _: (0, i, 0, 0))
    return tuple(
        call(
            functools.partial(finish_kernel, blocks, snps),
            idx,
            (row_stat, own_stat, mate_stat, ld_all, w_sums, *pairs),
            [stat_spec] * 3
            + [ld_spec, pl.BlockSpec((blocks, 3, tile, wide), lambda i, _: (0, 0, i, 0))]
            + [pl.BlockSpec((2, tile, wide), lambda i, _: (0, i, 0))] * blocks,
            [out, out],
            [out_spec, out_spec],
            grid=(width // tile,),
        )
    )
def general_device(ldscore, zscores):
    blocks = lax.axis_size("genome")
    grid_rows = lax.axis_size("trow")
    grid_cols = lax.axis_size("tcol")
    snp_count = zscores.shape[0]
    shard_width = zscores.shape[1]
    traits = shard_width * grid_rows * grid_cols
    row_width = traits // grid_rows
    row_share = row_width // blocks
    row_index = lax.axis_index("trow")
    col_index = lax.axis_index("tcol")
    genome_index = lax.axis_index("genome")
    ld_weight = 1.0 / ldscore
    z_float = zscores.astype(jnp.float32)
    z_square = z_float * z_float
    own_stats = jnp.stack(
        [jnp.sum(z_square * ld_weight[:, None], axis=0), jnp.sum(z_square, axis=0)]
    )
    own_scalars = jnp.stack([jnp.sum(ld_weight), jnp.sum(ldscore)])
    all_stats, all_scalars = (
        lax.all_gather(own_stats[None], ("genome", "trow", "tcol"), axis=0, tiled=True),
        lax.all_gather(own_scalars[None], ("genome", "trow", "tcol"), axis=0, tiled=True),
    )
    all_stats = all_stats.reshape(blocks, grid_rows * grid_cols, 2, shard_width)
    all_stats = all_stats.transpose(0, 2, 1, 3).reshape(blocks, 2, traits)
    all_scalars = all_scalars.reshape(blocks, grid_rows * grid_cols, 2)[:, 0, :]
    total_stats = jnp.sum(all_stats, axis=0)
    total_scalars = jnp.sum(all_scalars, axis=0)
    herit_full = slope_fit(
        total_scalars[0],
        total_scalars[1],
        total_stats[0],
        total_stats[1],
        float(snp_count * blocks),
    )
    rest_stats = total_stats[None] - all_stats
    rest_scalars = total_scalars[None] - all_scalars
    herit_del = slope_fit(
        rest_scalars[:, 0:1],
        rest_scalars[:, 1:2],
        rest_stats[:, 0],
        rest_stats[:, 1],
        float(snp_count * (blocks - 1)),
    )
    herit_pos = jnp.maximum(herit_full, 0.0)
    col_z = lax.all_gather(zscores, "trow", axis=1, tiled=True)
    col_herit = lax.dynamic_index_in_dim(
        herit_pos.reshape(grid_rows, grid_cols, shard_width), col_index, 1, keepdims=False
    ).reshape(-1)
    col_u = weights_for(col_herit, ldscore)
    col_zu = (col_z.astype(jnp.float32) * col_u.astype(jnp.float32)).astype(jnp.bfloat16)
    piece = lax.all_gather(zscores, "tcol", axis=1, tiled=True)
    herit_rows = lax.dynamic_slice_in_dim(herit_pos, row_index * row_width, piece.shape[1])
    row_u = weights_for(herit_rows, ldscore)
    u_float = row_u.astype(jnp.float32)
    scaled = piece.astype(jnp.float32) * u_float
    row_zu = scaled.astype(jnp.bfloat16)
    row_scaled = (scaled * ld_weight[:, None]).astype(jnp.bfloat16)
    products = [contract(row_scaled, col_zu), contract(row_zu, col_zu)]
    row_inv = (u_float * ld_weight[:, None]).astype(jnp.bfloat16)
    row_ld = (u_float * ldscore[:, None]).astype(jnp.bfloat16)
    products = products + [
        contract(row_inv, col_u),
        contract(row_u, col_u),
        contract(row_ld, col_u),
    ]
    sums = jnp.stack(products)
    sums = sums.astype(jnp.bfloat16)[:, None]
    row_start = row_index * row_width + genome_index * row_share
    tiles = lax.all_to_all(sums, "genome", split_axis=2, concat_axis=1, tiled=True)
    tile_values = tiles.astype(jnp.float32)
    totals = jnp.sum(tile_values, axis=1)
    deleted = totals[:, None] - tile_values
    full_g = coupling(totals)
    del_g = coupling(deleted)
    herit_floor = jnp.maximum(herit_full, floor_value)
    del_floor = jnp.maximum(herit_del, floor_value)
    rows_full = lax.dynamic_slice_in_dim(herit_floor, row_start, row_share)
    cols_full = lax.dynamic_index_in_dim(
        herit_floor.reshape(grid_rows, grid_cols, shard_width), col_index, 1, keepdims=False
    ).reshape(-1)
    rows_del = lax.dynamic_slice_in_dim(del_floor, row_start, row_share, axis=1)
    cols_del = lax.dynamic_index_in_dim(
        del_floor.reshape(blocks, grid_rows, grid_cols, shard_width), col_index, 2, keepdims=False
    ).reshape(blocks, -1)
    rg_tile = full_g / jnp.sqrt(rows_full[:, None] * cols_full[None, :])
    rg_del = del_g / jnp.sqrt(rows_del[:, :, None] * cols_del[:, None, :])
    mean_del = jnp.mean(rg_del, axis=0)
    differ = rg_del - mean_del[None]
    spread = jnp.sum(differ * differ, axis=0)
    se_tile = jnp.sqrt((blocks - 1) / blocks * spread)
    out_shape = (1, row_share, grid_rows, shard_width)
    return (rg_tile.reshape(out_shape), se_tile.reshape(out_shape))


def solution(mesh):
    sizes = tuple(mesh.shape[name] for name in axes)

    def per_device(ldscore, zscores):
        snps, width = zscores.shape
        square = sizes[0] == sizes[2] == 4 and sizes[1] == 2 and width % lanes == 0
        if square and snps % width == 0 and snps // sizes[2] % lanes == 0:
            return square_device(sizes, ldscore, zscores)
        return general_device(ldscore, zscores)

    return jax.shard_map(
        per_device,
        mesh=mesh,
        in_specs=(P("genome"), P("genome", ("trow", "tcol"))),
        out_specs=(P("trow", "genome", None, "tcol"), P("trow", "genome", None, "tcol")),
        check_vma=False,
    )
```

```python
import functools

import jax
import jax.numpy as jnp
from jax import lax
from jax.experimental import pallas as pl
from jax.experimental.pallas import tpu as pltpu
from jax.sharding import PartitionSpec as P


floor_value = 0.002
axes = ("genome", "trow", "tcol")
bf16 = jnp.bfloat16
f32 = jnp.float32
lanes = 128
vmem_bytes = 56 << 20


def contract(left, right):
    return lax.dot_general(
        left, right, (((0,), (0,)), ((), ())), preferred_element_type=f32
    )


def slope_fit(inv_sum, ld_sum, y_sum, l_sum, count):
    return (inv_sum * l_sum - count * y_sum) / (inv_sum * ld_sum - count * count)


def weights_for(herit_pos, ld_column):
    return (1.0 / (1.0 + herit_pos[None, :] * ld_column[:, None])).astype(bf16)


def coupling(tiles):
    return (tiles[2] * tiles[1] - tiles[3] * tiles[0]) / (tiles[2] * tiles[4] - tiles[3] * tiles[3])


def down_sublanes(row):
    return jnp.transpose(jnp.broadcast_to(row, (lanes, lanes)))


def widen(column, width):
    return jnp.concatenate([column] * (width // lanes), axis=1)


def message_kernel(parts, idx, z_ref, ld_ref, stat_ref, *outs):
    snps, width = z_ref.shape
    piece = width // parts
    for step, out in enumerate(outs):
        quarter = jnp.bitwise_xor(idx[2], step)
        out[...] = z_ref[:, pl.ds(pl.multiple_of(quarter * piece, piece), piece)]
    y_acc = jnp.zeros((8, width), f32)
    l_acc = jnp.zeros((8, width), f32)
    for chunk in range(snps // lanes):
        weight = widen(down_sublanes(1.0 / ld_ref[chunk : chunk + 1, :]), width)
        values = z_ref[chunk * lanes : (chunk + 1) * lanes, :].astype(f32)
        square = values * values
        l_acc = l_acc + jnp.sum(square.reshape(lanes // 8, 8, width), axis=0)
        y_acc = y_acc + jnp.sum((square * weight).reshape(lanes // 8, 8, width), axis=0)
    rows = [jnp.sum(y_acc, axis=0, keepdims=True), jnp.sum(l_acc, axis=0, keepdims=True)]
    step = width // lanes
    for row in range(snps // width):
        rows.append(jnp.concatenate([ld_ref[row * step + k : row * step + k + 1, :] for k in range(step)], axis=1))
    used = len(rows)
    stat_ref[...] = jnp.concatenate(rows + [jnp.zeros((stat_ref.shape[0] - used, width), f32)], axis=0)


def gather_kernel(parts, ld_rows, idx, *refs):
    ins, cols, (stat_ref, own_ref, ld_ref) = refs[:parts], refs[parts : 2 * parts], refs[2 * parts :]
    for step in range(parts):
        for source, out_ref, place in ((ins, stat_ref, idx[2]), (cols, own_ref, idx[0])):
            block = lax.rem(place + parts - step, parts)
            out_ref[pl.ds(block, 1), :] = source[step][0:1, :]
            out_ref[pl.ds(parts + block, 1), :] = source[step][1:2, :]
        block = lax.rem(idx[2] + parts - step, parts)
        for row in range(ld_rows):
            ld_ref[pl.ds(block * ld_rows + row, 1), :] = ins[step][2 + row : 3 + row, :]


def route_kernel(parts, idx, *refs):
    ins, outs = refs[:parts], refs[parts:]
    for shift in range(parts):
        chosen = jnp.bitwise_xor(idx[2], lax.rem(idx[0] + shift, parts))
        for step in range(parts):

            @pl.when(chosen == step)
            def _(shift=shift, step=step):
                outs[shift][...] = ins[step][...]


def join_kernel(idx, *refs):
    ins, out_ref = refs[:-1], refs[-1]
    for place, ref in enumerate(ins):
        out_ref[place] = ref[...]


def total(values):
    return jnp.sum(jnp.sum(values, axis=1, keepdims=True), axis=0, keepdims=True)


def herit_full(stats, ld, blocks, snps):
    inv = total(1.0 / ld)
    return slope_fit(
        inv,
        total(ld),
        jnp.sum(stats[:blocks], axis=0, keepdims=True),
        jnp.sum(stats[blocks:], axis=0, keepdims=True),
        float(snps * blocks),
    )


def herit_without(stats, ld, block, blocks, snps):
    per = ld.shape[0] // blocks
    inv = [total(1.0 / ld[b * per : (b + 1) * per]) for b in range(blocks)]
    lds = [total(ld[b * per : (b + 1) * per]) for b in range(blocks)]
    y_total = jnp.sum(stats[:blocks], axis=0, keepdims=True)
    l_total = jnp.sum(stats[blocks:], axis=0, keepdims=True)
    inv_total, ld_total = sum(inv[1:], inv[0]), sum(lds[1:], lds[0])
    return slope_fit(
        inv_total - inv[block],
        ld_total - lds[block],
        y_total - stats[block : block + 1],
        l_total - stats[blocks + block : blocks + block + 1],
        float(snps * (blocks - 1)),
    )


def scale_of(herit):
    return lax.rsqrt(jnp.maximum(herit, floor_value))


def all_scales(stats, ld, blocks, snps):
    scales = [scale_of(herit_full(stats, ld, blocks, snps))]
    return scales + [scale_of(herit_without(stats, ld, b, blocks, snps)) for b in range(blocks)]


def weight_kernel(blocks, begin, kept, idx, row_stat, own_stat, mate_stat, ld_ref, *refs):
    sums_ref, urow_ref, ucol_ref, invcol_ref, inv_ref, wld_ref = refs[kept:]
    snps, width = urow_ref.shape
    block = idx[3 + begin + pl.program_id(0)]
    ld = ld_ref[...]
    side = idx[1]
    here = [pl.multiple_of(side * width, width), pl.multiple_of((1 - side) * width, width)]
    herit_row = jnp.maximum(herit_full(row_stat[...], ld, blocks, snps), 0.0)
    herit_col = [
        jnp.maximum(herit_full(stat[...], ld, blocks, snps), 0.0) for stat in (own_stat, mate_stat)
    ]
    per = snps // width
    step = width // lanes
    row_of = lax.broadcasted_iota(jnp.int32, ld.shape, 0)
    here_ld = [
        jnp.sum(jnp.where(row_of == block * per + k, ld, 0.0), axis=0, keepdims=True) for k in range(per)
    ]
    for chunk in range(snps // lanes):
        at = slice(chunk * lanes, (chunk + 1) * lanes)
        column = down_sublanes(here_ld[chunk // step][:, (chunk % step) * lanes : (chunk % step + 1) * lanes])
        inv_column = 1.0 / column
        invcol_ref[at, :] = inv_column
        ld_wide = widen(column, width)
        inv_wide = widen(inv_column, width)
        u_row = (1.0 / (1.0 + herit_row * ld_wide)).astype(bf16)
        urow_ref[at, :] = u_row
        u_float = u_row.astype(f32)
        inv_ref[at, :] = (u_float * inv_wide).astype(bf16)
        wld_ref[at, :] = (u_float * ld_wide).astype(bf16)
        for half in range(2):
            ucol_ref[at, pl.ds(here[half], width)] = (
                1.0 / (1.0 + herit_col[half] * ld_wide)
            ).astype(bf16)
    u_col = ucol_ref[...]
    sums_ref[0] = contract(inv_ref[...], u_col).astype(bf16)
    sums_ref[1] = contract(urow_ref[...], u_col).astype(bf16)
    sums_ref[2] = contract(wld_ref[...], u_col).astype(bf16)


def weigh_columns(side, own_ref, mate_ref, ucol, place_ref):
    width = own_ref.shape[1]
    for half, ref in enumerate((own_ref, mate_ref)):
        place = side if half == 0 else 1 - side
        at = pl.ds(pl.multiple_of(place * width, width), width)
        place_ref[:, at] = ref[...] * ucol[:, at]


def weigh_rows(rows, urow, invcol, zu_ref, zinv_ref):
    snps, width = rows.shape
    for chunk in range(snps // lanes):
        at = slice(chunk * lanes, (chunk + 1) * lanes)
        scaled = rows[at, :].astype(f32) * urow[at, :].astype(f32)
        zu_ref[at, :] = scaled.astype(bf16)
        zinv_ref[at, :] = (scaled * widen(invcol[at, :], width)).astype(bf16)


def chosen(values, which):
    picked = values[0]
    for place in range(1, len(values)):
        picked = jnp.where(which == place, values[place], picked)
    return picked


def finish_kernel(parts, blocks, idx, *refs):
    first, pieces, refs = refs[:parts], refs[parts : 2 * parts], refs[2 * parts :]
    own, mate, refs = refs[:blocks], refs[blocks : 2 * blocks], refs[2 * blocks :]
    urow_hbm, ucol_hbm, inv_hbm, w_hbm, row_stat, own_stat, mate_stat, ld_ref, rg_ref, se_ref = refs[:10]
    rows_v, own_v, mate_v, urow_v, ucol_v, inv_v, zu_v, zinv_v, zcol_v, y_v, w_v, rs_v, cs_v, sems, w_sem = refs[10:]
    piece = first[0].shape[1]
    tile, width = rg_ref.shape[1], rg_ref.shape[3]
    snps = own[0].shape[0]
    side = idx[1]
    step_id = pl.program_id(0)
    w_copy = pltpu.make_async_copy(w_hbm, w_v, w_sem.at[0])

    @pl.when(step_id == 0)
    def _():
        copies = []
        for slot in range(blocks):
            turn = slot % 2
            mine = [
                (ucol_hbm.at[slot], ucol_v.at[turn]),
                (own[slot], own_v.at[turn]),
                (mate[slot], mate_v.at[turn]),
                (urow_hbm.at[slot], urow_v.at[turn]),
                (inv_hbm.at[slot], inv_v.at[turn]),
            ]
            for step in range(parts):
                start = pl.multiple_of(jnp.bitwise_xor(idx[2], step) * piece, piece)
                source = pieces[step].at[idx[3 + parts + slot]] if slot else first[step]
                mine.append((source, rows_v.at[turn, :, pl.ds(start, piece)]))
            copies.append([pltpu.make_async_copy(p, q, sems.at[slot, k]) for k, (p, q) in enumerate(mine)])

        def load(slot):
            if slot < blocks:
                for copy in copies[slot]:
                    copy.start()

        def prepare(slot):
            if slot < blocks:
                for copy in copies[slot]:
                    copy.wait()
                turn = slot % 2
                weigh_columns(side, own_v.at[turn], mate_v.at[turn], ucol_v.at[turn], zcol_v.at[turn])
                weigh_rows(rows_v.at[turn], urow_v.at[turn], inv_v.at[turn], zu_v.at[turn], zinv_v.at[turn])
                load(slot + 2)
                if slot == 1:
                    w_copy.start()

        load(0)
        load(1)
        ld = ld_ref[...]

        def scales(stat):
            values = all_scales(stat[...], ld, blocks, snps)
            return values[:1] + [chosen(values[1:], idx[3 + slot]) for slot in range(blocks)]

        for place, value in enumerate(scales(row_stat)):
            for chunk in range(width // lanes):
                rs_v[place, chunk * lanes : (chunk + 1) * lanes, :] = down_sublanes(
                    value[:, chunk * lanes : (chunk + 1) * lanes]
                )
        for place, (p, q) in enumerate(zip(scales(own_stat), scales(mate_stat))):
            cs_v[place : place + 1, :width] = jnp.where(side == 0, p, q)
            cs_v[place : place + 1, width:] = jnp.where(side == 0, q, p)
        prepare(0)
        for slot in range(blocks):
            prepare(slot + 1)
            turn = slot % 2
            z_col = zcol_v[turn]
            y_v[slot, 0] = contract(zinv_v[turn], z_col).astype(bf16)
            y_v[slot, 1] = contract(zu_v[turn], z_col).astype(bf16)

    @pl.when(step_id == 1)
    def _():
        w_copy.wait()

    @pl.when(step_id > 0)
    def _():
        start = pl.multiple_of((step_id - 1) * tile, tile)
        here = pl.ds(start, tile)
        for group in range(2 * width // lanes):
            at = slice(group * lanes, (group + 1) * lanes)
            half, inner = divmod(group * lanes, width)
            place = slice(inner, inner + lanes)
            t = [[y_v[s, k, here, at].astype(f32) for s in range(blocks)] for k in range(2)]
            t += [[w_v[s, k, here, at].astype(f32) for s in range(blocks)] for k in range(3)]
            sums = [sum(x[1:], x[0]) for x in t]
            values = []
            for s in range(blocks + 1):
                tiles = sums if s == 0 else [total_ - x[s - 1] for total_, x in zip(sums, t)]
                values.append(coupling(tiles) * (rs_v[s, here, :] * cs_v[s : s + 1, at]))
            rg_ref[0, :, half, place] = values[0]
            dels = values[1:]
            mean = sum(dels[1:], dels[0]) * (1.0 / blocks)
            spread = sum([(d - mean) * (d - mean) for d in dels[1:]], (dels[0] - mean) * (dels[0] - mean))
            se_ref[0, :, half, place] = jnp.sqrt((blocks - 1) / blocks * spread)


def whole(shape):
    return pl.BlockSpec(shape, lambda *_: (0,) * len(shape))


def call(kernel, idx, ins, in_specs, outs, out_specs, grid=(1,), scratch=(), flops=0, ops=0, aliases={}):
    moved = sum(x.size * x.dtype.itemsize for x in jax.tree.leaves((ins, outs)))
    return pl.pallas_call(
        kernel,
        input_output_aliases=aliases,
        grid_spec=pltpu.PrefetchScalarGridSpec(
            num_scalar_prefetch=1,
            grid=grid,
            in_specs=in_specs,
            out_specs=out_specs,
            scratch_shapes=list(scratch),
        ),
        out_shape=outs,
        compiler_params=pltpu.CompilerParams(vmem_limit_bytes=vmem_bytes),
        cost_estimate=pl.CostEstimate(flops=flops, transcendentals=ops, bytes_accessed=moved),
    )(idx, *ins)


def square_device(sizes, ldscore, zscores):
    blocks, grid_rows, parts = sizes
    snps, width = zscores.shape
    piece = width // parts
    g, r, c = (lax.axis_index(name) for name in axes)

    def move(value, target):
        pairs = []
        for gi in range(blocks):
            for ri in range(grid_rows):
                for ci in range(parts):
                    to = target(gi, ri, ci)
                    if to is not None:
                        source = (gi * grid_rows + ri) * parts + ci
                        pairs.append((source, (to[0] * grid_rows + to[1]) * parts + to[2]))
        return lax.ppermute(value, axes, pairs)

    def swap(value):
        return move(value, lambda gi, ri, ci: (gi, 1 - ri, ci))

    def line(value, table):
        return move(value, lambda gi, ri, ci: (table[gi], ri, ci) if gi in table else None)

    low = g < 2
    slot_blocks = [g, jnp.bitwise_xor(g, 1), jnp.where(low, 2, 1), jnp.where(low, 3, 0)]
    shifts = [lax.rem(g + blocks - b, blocks) - 1 for b in slot_blocks]
    idx = jnp.stack([g, r, c] + slot_blocks + shifts).astype(jnp.int32)

    near = line(zscores, {0: 1, 1: 0, 2: 3, 3: 2})
    inner = line(zscores, {1: 2, 2: 1})

    ld_rows = snps // width
    message = jax.ShapeDtypeStruct((snps, piece), bf16)
    note = jax.ShapeDtypeStruct((-(-(2 + ld_rows) // 8) * 8, width), f32)
    stat = jax.ShapeDtypeStruct((2 * blocks, width), f32)
    ld_shape = jax.ShapeDtypeStruct((blocks * ld_rows, width), f32)
    notes, *sent = call(
        functools.partial(message_kernel, parts),
        idx,
        (zscores, ldscore.reshape(snps // lanes, lanes)),
        [whole((snps, width)), whole((snps // lanes, lanes))],
        [note] + [message] * parts,
        [whole(note.shape)] + [whole(message.shape)] * parts,
    )
    told = [move(notes, lambda gi, ri, ci, step=step: (ci, ri, (gi + step) % parts)) for step in range(parts)]
    seen = [notes] + [line(notes, {gi: (gi + step) % blocks for gi in range(blocks)}) for step in range(1, blocks)]
    held = [sent[0]] + [move(sent[step], lambda gi, ri, ci, step=step: (gi, ri, ci ^ step)) for step in range(1, parts)]
    row_stat, own_stat, ld_all = call(
        functools.partial(gather_kernel, parts, ld_rows),
        idx,
        (*told, *seen),
        [whole(note.shape)] * (2 * parts),
        [stat, stat, ld_shape],
        [whole(stat.shape), whole(stat.shape), whole(ld_shape.shape)],
    )
    mate_stat = swap(own_stat)
    routed = call(
        functools.partial(route_kernel, parts),
        idx,
        held,
        [whole(message.shape)] * parts,
        [message] * parts,
        [whole(message.shape)] * parts,
    )
    arrived = [line(routed[step], {gi: (gi + step) % blocks for gi in range(blocks)}) for step in range(1, blocks)]
    first = [routed[0]] + [
        move(routed[0], lambda gi, ri, ci, step=step: (gi, ri, ci ^ step)) for step in range(1, parts)
    ]
    joined = jax.ShapeDtypeStruct((blocks - 1, snps, piece), bf16)
    quarter_rows = call(
        join_kernel, idx, arrived, [whole(message.shape)] * (blocks - 1), joined, whole(joined.shape)
    )
    rows = [quarter_rows] + [
        move(quarter_rows, lambda gi, ri, ci, step=step: (gi, ri, ci ^ step)) for step in range(1, parts)
    ]
    stats = (row_stat, own_stat, mate_stat, ld_all)
    outer = line(inner, {1: 0, 2: 3})
    half = snps // 2
    cross = [line(near[k * half : (k + 1) * half], {1: 2, 2: 1}) for k in range(2)]
    last = [line(cross[k], {1: 0, 2: 3}) for k in range(2)]
    mate = [swap(zscores), swap(near)]

    stat_spec = whole(stat.shape)
    ld_spec = whole(ld_shape.shape)
    wide = grid_rows * width
    tile = lanes
    anyspec = pl.BlockSpec(memory_space=pl.ANY)
    stats = (row_stat, own_stat, mate_stat, ld_all)
    stat_specs = [stat_spec] * 3 + [ld_spec]
    held_weights = ()
    span = blocks // 2
    for k in range(2):
        kept = len(held_weights)
        spot = lambda i, _, k=k: (i + k * span, 0, 0)
        held_weights = call(
            functools.partial(weight_kernel, blocks, k * span, kept),
            idx,
            (*stats, *held_weights),
            stat_specs + [anyspec] * kept,
            [
                jax.ShapeDtypeStruct((blocks, 3, width, wide), bf16),
                jax.ShapeDtypeStruct((blocks, snps, width), bf16),
                jax.ShapeDtypeStruct((blocks, snps, wide), bf16),
                jax.ShapeDtypeStruct((blocks, snps, lanes), f32),
            ],
            [
                pl.BlockSpec((None, 3, width, wide), lambda i, _, k=k: (i + k * span, 0, 0, 0)),
                pl.BlockSpec((None, snps, width), spot),
                pl.BlockSpec((None, snps, wide), spot),
                pl.BlockSpec((None, snps, lanes), spot),
            ],
            grid=(span,),
            scratch=[pltpu.VMEM((snps, width), bf16)] * 2,
            flops=6 * span * snps * width * wide,
            aliases={5 + j: j for j in range(kept)},
        )
    w_sums, u_row, u_col, inv_col = held_weights
    outer, last[1], u_row = lax.optimization_barrier((outer, last[1], u_row))
    own = [zscores, near, inner + outer]
    own.append(jnp.concatenate([cross[k] + last[k] for k in range(2)], axis=0))
    mate = mate + [swap(own[slot]) for slot in (2, 3)]
    small = tile // 2
    out = jax.ShapeDtypeStruct((1, width, grid_rows, width), f32)
    out_spec = pl.BlockSpec((1, small, grid_rows, width), lambda i, _: (0, jnp.maximum(i - 1, 0), 0, 0))
    return tuple(
        call(
            functools.partial(finish_kernel, parts, blocks),
            idx,
            (*first, *rows, *own, *mate, u_row, u_col, inv_col, w_sums, *stats),
            [anyspec] * (2 * parts + 2 * blocks + 4) + stat_specs,
            [out, out],
            [out_spec, out_spec],
            grid=(1 + width // small,),
            scratch=[
                pltpu.VMEM((2, snps, width), bf16),
                pltpu.VMEM((2, snps, width), bf16),
                pltpu.VMEM((2, snps, width), bf16),
                pltpu.VMEM((2, snps, width), bf16),
                pltpu.VMEM((2, snps, wide), bf16),
                pltpu.VMEM((2, snps, lanes), f32),
                pltpu.VMEM((2, snps, width), bf16),
                pltpu.VMEM((2, snps, width), bf16),
                pltpu.VMEM((2, snps, wide), bf16),
                pltpu.VMEM((blocks, 2, width, wide), bf16),
                pltpu.VMEM((blocks, 3, width, wide), bf16),
                pltpu.VMEM((blocks + 1, width, lanes), f32),
                pltpu.VMEM((8, wide), f32),
                pltpu.SemaphoreType.DMA((blocks, 5 + parts)),
                pltpu.SemaphoreType.DMA((1,)),
            ],
            flops=4 * blocks * snps * width * wide,
        )
    )


def general_device(ldscore, zscores):
    blocks = lax.axis_size("genome")
    grid_rows = lax.axis_size("trow")
    grid_cols = lax.axis_size("tcol")
    snp_count = zscores.shape[0]
    shard_width = zscores.shape[1]
    traits = shard_width * grid_rows * grid_cols
    row_width = traits // grid_rows
    row_share = row_width // blocks
    row_index = lax.axis_index("trow")
    col_index = lax.axis_index("tcol")
    genome_index = lax.axis_index("genome")
    ld_weight = 1.0 / ldscore
    z_float = zscores.astype(jnp.float32)
    z_square = z_float * z_float
    own_stats = jnp.stack(
        [jnp.sum(z_square * ld_weight[:, None], axis=0), jnp.sum(z_square, axis=0)]
    )
    own_scalars = jnp.stack([jnp.sum(ld_weight), jnp.sum(ldscore)])
    all_stats, all_scalars = (
        lax.all_gather(own_stats[None], ("genome", "trow", "tcol"), axis=0, tiled=True),
        lax.all_gather(own_scalars[None], ("genome", "trow", "tcol"), axis=0, tiled=True),
    )
    all_stats = all_stats.reshape(blocks, grid_rows * grid_cols, 2, shard_width)
    all_stats = all_stats.transpose(0, 2, 1, 3).reshape(blocks, 2, traits)
    all_scalars = all_scalars.reshape(blocks, grid_rows * grid_cols, 2)[:, 0, :]
    total_stats = jnp.sum(all_stats, axis=0)
    total_scalars = jnp.sum(all_scalars, axis=0)
    herit_full = slope_fit(
        total_scalars[0],
        total_scalars[1],
        total_stats[0],
        total_stats[1],
        float(snp_count * blocks),
    )
    rest_stats = total_stats[None] - all_stats
    rest_scalars = total_scalars[None] - all_scalars
    herit_del = slope_fit(
        rest_scalars[:, 0:1],
        rest_scalars[:, 1:2],
        rest_stats[:, 0],
        rest_stats[:, 1],
        float(snp_count * (blocks - 1)),
    )
    herit_pos = jnp.maximum(herit_full, 0.0)
    col_z = lax.all_gather(zscores, "trow", axis=1, tiled=True)
    col_herit = lax.dynamic_index_in_dim(
        herit_pos.reshape(grid_rows, grid_cols, shard_width), col_index, 1, keepdims=False
    ).reshape(-1)
    col_u = weights_for(col_herit, ldscore)
    col_zu = (col_z.astype(jnp.float32) * col_u.astype(jnp.float32)).astype(jnp.bfloat16)
    piece = lax.all_gather(zscores, "tcol", axis=1, tiled=True)
    herit_rows = lax.dynamic_slice_in_dim(herit_pos, row_index * row_width, piece.shape[1])
    row_u = weights_for(herit_rows, ldscore)
    u_float = row_u.astype(jnp.float32)
    scaled = piece.astype(jnp.float32) * u_float
    row_zu = scaled.astype(jnp.bfloat16)
    row_scaled = (scaled * ld_weight[:, None]).astype(jnp.bfloat16)
    products = [contract(row_scaled, col_zu), contract(row_zu, col_zu)]
    row_inv = (u_float * ld_weight[:, None]).astype(jnp.bfloat16)
    row_ld = (u_float * ldscore[:, None]).astype(jnp.bfloat16)
    products = products + [
        contract(row_inv, col_u),
        contract(row_u, col_u),
        contract(row_ld, col_u),
    ]
    sums = jnp.stack(products)
    sums = sums.astype(jnp.bfloat16)[:, None]
    row_start = row_index * row_width + genome_index * row_share
    tiles = lax.all_to_all(sums, "genome", split_axis=2, concat_axis=1, tiled=True)
    tile_values = tiles.astype(jnp.float32)
    totals = jnp.sum(tile_values, axis=1)
    deleted = totals[:, None] - tile_values
    full_g = coupling(totals)
    del_g = coupling(deleted)
    herit_floor = jnp.maximum(herit_full, floor_value)
    del_floor = jnp.maximum(herit_del, floor_value)
    rows_full = lax.dynamic_slice_in_dim(herit_floor, row_start, row_share)
    cols_full = lax.dynamic_index_in_dim(
        herit_floor.reshape(grid_rows, grid_cols, shard_width), col_index, 1, keepdims=False
    ).reshape(-1)
    rows_del = lax.dynamic_slice_in_dim(del_floor, row_start, row_share, axis=1)
    cols_del = lax.dynamic_index_in_dim(
        del_floor.reshape(blocks, grid_rows, grid_cols, shard_width), col_index, 2, keepdims=False
    ).reshape(blocks, -1)
    rg_tile = full_g / jnp.sqrt(rows_full[:, None] * cols_full[None, :])
    rg_del = del_g / jnp.sqrt(rows_del[:, :, None] * cols_del[:, None, :])
    mean_del = jnp.mean(rg_del, axis=0)
    differ = rg_del - mean_del[None]
    spread = jnp.sum(differ * differ, axis=0)
    se_tile = jnp.sqrt((blocks - 1) / blocks * spread)
    out_shape = (1, row_share, grid_rows, shard_width)
    return (rg_tile.reshape(out_shape), se_tile.reshape(out_shape))


def is_square(sizes):
    return sizes[0] == sizes[2] == 4 and sizes[1] == 2


def solution(mesh):
    sizes = tuple(mesh.shape[name] for name in axes)

    def per_device(ldscore, zscores):
        snps, width = zscores.shape
        if is_square(sizes) and width % lanes == 0 and snps % width == 0 and width // sizes[2] % lanes == 0 and snps % (2 * lanes) == 0:
            return square_device(sizes, ldscore, zscores)
        return general_device(ldscore, zscores)

    step = jax.shard_map(
        per_device,
        mesh=mesh,
        in_specs=(P("genome"), P("genome", ("trow", "tcol"))),
        out_specs=(P("trow", "genome", None, "tcol"), P("trow", "genome", None, "tcol")),
        check_vma=False,
    )
    return step if is_square(sizes) else step
```

```python
import functools

import jax
import jax.numpy as jnp
from jax import lax
from jax.experimental import pallas as pl
from jax.experimental.pallas import tpu as pltpu
from jax.sharding import PartitionSpec as P


floor_value = 0.002
axes = ("genome", "trow", "tcol")
bf16 = jnp.bfloat16
f32 = jnp.float32
lanes = 128
vmem_bytes = 56 << 20


def contract(left, right):
    return lax.dot_general(
        left, right, (((0,), (0,)), ((), ())), preferred_element_type=f32
    )


def slope_fit(inv_sum, ld_sum, y_sum, l_sum, count):
    return (inv_sum * l_sum - count * y_sum) / (inv_sum * ld_sum - count * count)


def weights_for(herit_pos, ld_column):
    return (1.0 / (1.0 + herit_pos[None, :] * ld_column[:, None])).astype(bf16)


def coupling(tiles):
    return (tiles[2] * tiles[1] - tiles[3] * tiles[0]) / (tiles[2] * tiles[4] - tiles[3] * tiles[3])


def down_sublanes(row):
    return jnp.transpose(jnp.broadcast_to(row, (lanes, lanes)))


def widen(column, width):
    return jnp.concatenate([column] * (width // lanes), axis=1)


def message_kernel(parts, idx, z_ref, ld_ref, stat_ref, *outs):
    snps, width = z_ref.shape
    piece = width // parts
    for step, out in enumerate(outs):
        quarter = jnp.bitwise_xor(idx[2], step)
        out[...] = z_ref[:, pl.ds(pl.multiple_of(quarter * piece, piece), piece)]
    y_acc = jnp.zeros((8, width), f32)
    l_acc = jnp.zeros((8, width), f32)
    for chunk in range(snps // lanes):
        weight = widen(down_sublanes(1.0 / ld_ref[chunk : chunk + 1, :]), width)
        values = z_ref[chunk * lanes : (chunk + 1) * lanes, :].astype(f32)
        square = values * values
        l_acc = l_acc + jnp.sum(square.reshape(lanes // 8, 8, width), axis=0)
        y_acc = y_acc + jnp.sum((square * weight).reshape(lanes // 8, 8, width), axis=0)
    rows = [jnp.sum(y_acc, axis=0, keepdims=True), jnp.sum(l_acc, axis=0, keepdims=True)]
    step = width // lanes
    for row in range(snps // width):
        rows.append(jnp.concatenate([ld_ref[row * step + k : row * step + k + 1, :] for k in range(step)], axis=1))
    used = len(rows)
    stat_ref[...] = jnp.concatenate(rows + [jnp.zeros((stat_ref.shape[0] - used, width), f32)], axis=0)


def gather_kernel(parts, ld_rows, idx, *refs):
    ins, cols, (stat_ref, own_ref, ld_ref) = refs[:parts], refs[parts : 2 * parts], refs[2 * parts :]
    for step in range(parts):
        for source, out_ref, place in ((ins, stat_ref, idx[2]), (cols, own_ref, idx[0])):
            block = lax.rem(place + parts - step, parts)
            out_ref[pl.ds(block, 1), :] = source[step][0:1, :]
            out_ref[pl.ds(parts + block, 1), :] = source[step][1:2, :]
        block = lax.rem(idx[2] + parts - step, parts)
        for row in range(ld_rows):
            ld_ref[pl.ds(block * ld_rows + row, 1), :] = ins[step][2 + row : 3 + row, :]


def route_kernel(parts, idx, *refs):
    ins, outs = refs[:parts], refs[parts:]
    for shift in range(parts):
        chosen = jnp.bitwise_xor(idx[2], lax.rem(idx[0] + shift, parts))
        for step in range(parts):

            @pl.when(chosen == step)
            def _(shift=shift, step=step):
                outs[shift][...] = ins[step][...]


def join_kernel(idx, *refs):
    ins, out_ref = refs[:-1], refs[-1]
    for place, ref in enumerate(ins):
        out_ref[place] = ref[...]


def total(values):
    return jnp.sum(jnp.sum(values, axis=1, keepdims=True), axis=0, keepdims=True)


def herit_full(stats, ld, blocks, snps):
    inv = total(1.0 / ld)
    return slope_fit(
        inv,
        total(ld),
        jnp.sum(stats[:blocks], axis=0, keepdims=True),
        jnp.sum(stats[blocks:], axis=0, keepdims=True),
        float(snps * blocks),
    )


def herit_without(stats, ld, block, blocks, snps):
    per = ld.shape[0] // blocks
    inv = [total(1.0 / ld[b * per : (b + 1) * per]) for b in range(blocks)]
    lds = [total(ld[b * per : (b + 1) * per]) for b in range(blocks)]
    y_total = jnp.sum(stats[:blocks], axis=0, keepdims=True)
    l_total = jnp.sum(stats[blocks:], axis=0, keepdims=True)
    inv_total, ld_total = sum(inv[1:], inv[0]), sum(lds[1:], lds[0])
    return slope_fit(
        inv_total - inv[block],
        ld_total - lds[block],
        y_total - stats[block : block + 1],
        l_total - stats[blocks + block : blocks + block + 1],
        float(snps * (blocks - 1)),
    )


def scale_of(herit):
    return lax.rsqrt(jnp.maximum(herit, floor_value))


def all_scales(stats, ld, blocks, snps):
    scales = [scale_of(herit_full(stats, ld, blocks, snps))]
    return scales + [scale_of(herit_without(stats, ld, b, blocks, snps)) for b in range(blocks)]


def weight_kernel(blocks, begin, kept, idx, row_stat, own_stat, mate_stat, ld_ref, *refs):
    sums_ref, urow_ref, ucol_ref, invcol_ref, inv_ref, wld_ref = refs[kept:]
    snps, width = urow_ref.shape
    block = idx[3 + begin + pl.program_id(0)]
    ld = ld_ref[...]
    side = idx[1]
    here = [pl.multiple_of(side * width, width), pl.multiple_of((1 - side) * width, width)]
    herit_row = jnp.maximum(herit_full(row_stat[...], ld, blocks, snps), 0.0)
    herit_col = [
        jnp.maximum(herit_full(stat[...], ld, blocks, snps), 0.0) for stat in (own_stat, mate_stat)
    ]
    per = snps // width
    step = width // lanes
    row_of = lax.broadcasted_iota(jnp.int32, ld.shape, 0)
    here_ld = [
        jnp.sum(jnp.where(row_of == block * per + k, ld, 0.0), axis=0, keepdims=True) for k in range(per)
    ]
    for chunk in range(snps // lanes):
        at = slice(chunk * lanes, (chunk + 1) * lanes)
        column = down_sublanes(here_ld[chunk // step][:, (chunk % step) * lanes : (chunk % step + 1) * lanes])
        inv_column = 1.0 / column
        invcol_ref[at, :] = inv_column
        ld_wide = widen(column, width)
        inv_wide = widen(inv_column, width)
        u_row = (1.0 / (1.0 + herit_row * ld_wide)).astype(bf16)
        urow_ref[at, :] = u_row
        u_float = u_row.astype(f32)
        inv_ref[at, :] = (u_float * inv_wide).astype(bf16)
        wld_ref[at, :] = (u_float * ld_wide).astype(bf16)
        for half in range(2):
            ucol_ref[at, pl.ds(here[half], width)] = (
                1.0 / (1.0 + herit_col[half] * ld_wide)
            ).astype(bf16)
    u_col = ucol_ref[...]
    sums_ref[0] = contract(inv_ref[...], u_col).astype(bf16)
    sums_ref[1] = contract(urow_ref[...], u_col).astype(bf16)
    sums_ref[2] = contract(wld_ref[...], u_col).astype(bf16)


def weigh_columns(side, own_ref, mate_ref, ucol, place_ref):
    width = own_ref.shape[1]
    for half, ref in enumerate((own_ref, mate_ref)):
        place = side if half == 0 else 1 - side
        at = pl.ds(pl.multiple_of(place * width, width), width)
        place_ref[:, at] = ref[...] * ucol[:, at]


def weigh_rows(rows, urow, invcol, zu_ref, zinv_ref):
    snps, width = rows.shape
    for chunk in range(snps // lanes):
        at = slice(chunk * lanes, (chunk + 1) * lanes)
        scaled = rows[at, :].astype(f32) * urow[at, :].astype(f32)
        zu_ref[at, :] = scaled.astype(bf16)
        zinv_ref[at, :] = (scaled * widen(invcol[at, :], width)).astype(bf16)


def chosen(values, which):
    picked = values[0]
    for place in range(1, len(values)):
        picked = jnp.where(which == place, values[place], picked)
    return picked


def finish_kernel(parts, blocks, idx, *refs):
    first, pieces, refs = refs[:parts], refs[parts : 2 * parts], refs[2 * parts :]
    own, mate, refs = refs[:blocks], refs[blocks : 2 * blocks], refs[2 * blocks :]
    urow_hbm, ucol_hbm, inv_hbm, w_hbm, row_stat, own_stat, mate_stat, ld_ref, rg_ref, se_ref = refs[:10]
    rows_v, own_v, mate_v, urow_v, ucol_v, inv_v, zu_v, zinv_v, zcol_v, y_v, w_v, rs_v, cs_v, sems, w_sem = refs[10:]
    piece = first[0].shape[1]
    snps, width = own[0].shape
    stride = 2 * width // lanes
    tile = rg_ref.shape[0] // stride
    side = idx[1]
    step_id = pl.program_id(0)
    w_copy = pltpu.make_async_copy(w_hbm, w_v, w_sem.at[0])

    @pl.when(step_id == 0)
    def _():
        copies = []
        for slot in range(blocks):
            turn = slot % 2
            mine = [
                (ucol_hbm.at[slot], ucol_v.at[turn]),
                (own[slot], own_v.at[turn]),
                (mate[slot], mate_v.at[turn]),
                (urow_hbm.at[slot], urow_v.at[turn]),
                (inv_hbm.at[slot], inv_v.at[turn]),
            ]
            for step in range(parts):
                start = pl.multiple_of(jnp.bitwise_xor(idx[2], step) * piece, piece)
                source = pieces[step].at[idx[3 + parts + slot]] if slot else first[step]
                mine.append((source, rows_v.at[turn, :, pl.ds(start, piece)]))
            copies.append([pltpu.make_async_copy(p, q, sems.at[slot, k]) for k, (p, q) in enumerate(mine)])

        def load(slot):
            if slot < blocks:
                for copy in copies[slot]:
                    copy.start()

        def prepare(slot):
            if slot < blocks:
                for copy in copies[slot]:
                    copy.wait()
                turn = slot % 2
                weigh_columns(side, own_v.at[turn], mate_v.at[turn], ucol_v.at[turn], zcol_v.at[turn])
                weigh_rows(rows_v.at[turn], urow_v.at[turn], inv_v.at[turn], zu_v.at[turn], zinv_v.at[turn])
                load(slot + 2)
                if slot == 1:
                    w_copy.start()

        load(0)
        load(1)
        ld = ld_ref[...]

        def scales(stat):
            values = all_scales(stat[...], ld, blocks, snps)
            return values[:1] + [chosen(values[1:], idx[3 + slot]) for slot in range(blocks)]

        for place, value in enumerate(scales(row_stat)):
            for chunk in range(width // lanes):
                rs_v[place, chunk * lanes : (chunk + 1) * lanes, :] = down_sublanes(
                    value[:, chunk * lanes : (chunk + 1) * lanes]
                )
        for place, (p, q) in enumerate(zip(scales(own_stat), scales(mate_stat))):
            cs_v[place : place + 1, :width] = jnp.where(side == 0, p, q)
            cs_v[place : place + 1, width:] = jnp.where(side == 0, q, p)
        prepare(0)
        for slot in range(blocks):
            prepare(slot + 1)
            turn = slot % 2
            z_col = zcol_v[turn]
            y_v[slot, 0] = contract(zinv_v[turn], z_col).astype(bf16)
            y_v[slot, 1] = contract(zu_v[turn], z_col).astype(bf16)

    @pl.when(step_id == 1)
    def _():
        w_copy.wait()

    @pl.when(step_id > 0)
    def _():
        start = pl.multiple_of((step_id - 1) * tile, tile)
        here = pl.ds(start, tile)
        for group in range(2 * width // lanes):
            at = slice(group * lanes, (group + 1) * lanes)
            half, inner = divmod(group * lanes, width)
            place = pl.ds(inner // lanes * 2 + half, tile, stride=stride)
            t = [[y_v[s, k, here, at].astype(f32) for s in range(blocks)] for k in range(2)]
            t += [[w_v[s, k, here, at].astype(f32) for s in range(blocks)] for k in range(3)]
            sums = [sum(x[1:], x[0]) for x in t]
            values = []
            for s in range(blocks + 1):
                tiles = sums if s == 0 else [total_ - x[s - 1] for total_, x in zip(sums, t)]
                values.append(coupling(tiles) * (rs_v[s, here, :] * cs_v[s : s + 1, at]))
            rg_ref[place, :] = values[0]
            dels = values[1:]
            mean = sum(dels[1:], dels[0]) * (1.0 / blocks)
            spread = sum([(d - mean) * (d - mean) for d in dels[1:]], (dels[0] - mean) * (dels[0] - mean))
            se_ref[place, :] = jnp.sqrt((blocks - 1) / blocks * spread)


def whole(shape):
    return pl.BlockSpec(shape, lambda *_: (0,) * len(shape))


def call(kernel, idx, ins, in_specs, outs, out_specs, grid=(1,), scratch=(), flops=0, ops=0, aliases={}):
    moved = sum(x.size * x.dtype.itemsize for x in jax.tree.leaves((ins, outs)))
    return pl.pallas_call(
        kernel,
        input_output_aliases=aliases,
        grid_spec=pltpu.PrefetchScalarGridSpec(
            num_scalar_prefetch=1,
            grid=grid,
            in_specs=in_specs,
            out_specs=out_specs,
            scratch_shapes=list(scratch),
        ),
        out_shape=outs,
        compiler_params=pltpu.CompilerParams(vmem_limit_bytes=vmem_bytes),
        cost_estimate=pl.CostEstimate(flops=flops, transcendentals=ops, bytes_accessed=moved),
    )(idx, *ins)


def square_device(sizes, ldscore, zscores):
    blocks, grid_rows, parts = sizes
    snps, width = zscores.shape
    piece = width // parts
    g, r, c = (lax.axis_index(name) for name in axes)

    def move(value, target):
        pairs = []
        for gi in range(blocks):
            for ri in range(grid_rows):
                for ci in range(parts):
                    to = target(gi, ri, ci)
                    if to is not None:
                        source = (gi * grid_rows + ri) * parts + ci
                        pairs.append((source, (to[0] * grid_rows + to[1]) * parts + to[2]))
        return lax.ppermute(value, axes, pairs)

    def swap(value):
        return move(value, lambda gi, ri, ci: (gi, 1 - ri, ci))

    def line(value, table):
        return move(value, lambda gi, ri, ci: (table[gi], ri, ci) if gi in table else None)

    low = g < 2
    slot_blocks = [g, jnp.bitwise_xor(g, 1), jnp.where(low, 2, 1), jnp.where(low, 3, 0)]
    shifts = [lax.rem(g + blocks - b, blocks) - 1 for b in slot_blocks]
    idx = jnp.stack([g, r, c] + slot_blocks + shifts).astype(jnp.int32)

    near = line(zscores, {0: 1, 1: 0, 2: 3, 3: 2})
    inner = line(zscores, {1: 2, 2: 1})

    ld_rows = snps // width
    message = jax.ShapeDtypeStruct((snps, piece), bf16)
    note = jax.ShapeDtypeStruct((-(-(2 + ld_rows) // 8) * 8, width), f32)
    stat = jax.ShapeDtypeStruct((2 * blocks, width), f32)
    ld_shape = jax.ShapeDtypeStruct((blocks * ld_rows, width), f32)
    notes, *sent = call(
        functools.partial(message_kernel, parts),
        idx,
        (zscores, ldscore.reshape(snps // lanes, lanes)),
        [whole((snps, width)), whole((snps // lanes, lanes))],
        [note] + [message] * parts,
        [whole(note.shape)] + [whole(message.shape)] * parts,
    )
    told = [move(notes, lambda gi, ri, ci, step=step: (ci, ri, (gi + step) % parts)) for step in range(parts)]
    seen = [notes] + [line(notes, {gi: (gi + step) % blocks for gi in range(blocks)}) for step in range(1, blocks)]
    held = [sent[0]] + [move(sent[step], lambda gi, ri, ci, step=step: (gi, ri, ci ^ step)) for step in range(1, parts)]
    row_stat, own_stat, ld_all = call(
        functools.partial(gather_kernel, parts, ld_rows),
        idx,
        (*told, *seen),
        [whole(note.shape)] * (2 * parts),
        [stat, stat, ld_shape],
        [whole(stat.shape), whole(stat.shape), whole(ld_shape.shape)],
    )
    mate_stat = swap(own_stat)
    routed = call(
        functools.partial(route_kernel, parts),
        idx,
        held,
        [whole(message.shape)] * parts,
        [message] * parts,
        [whole(message.shape)] * parts,
    )
    arrived = [line(routed[step], {gi: (gi + step) % blocks for gi in range(blocks)}) for step in range(1, blocks)]
    first = [routed[0]] + [
        move(routed[0], lambda gi, ri, ci, step=step: (gi, ri, ci ^ step)) for step in range(1, parts)
    ]
    joined = jax.ShapeDtypeStruct((blocks - 1, snps, piece), bf16)
    quarter_rows = call(
        join_kernel, idx, arrived, [whole(message.shape)] * (blocks - 1), joined, whole(joined.shape)
    )
    rows = [quarter_rows] + [
        move(quarter_rows, lambda gi, ri, ci, step=step: (gi, ri, ci ^ step)) for step in range(1, parts)
    ]
    stats = (row_stat, own_stat, mate_stat, ld_all)
    outer = line(inner, {1: 0, 2: 3})
    half = snps // 2
    cross = [line(near[k * half : (k + 1) * half], {1: 2, 2: 1}) for k in range(2)]
    last = [line(cross[k], {1: 0, 2: 3}) for k in range(2)]
    mate = [swap(zscores), swap(near)]

    stat_spec = whole(stat.shape)
    ld_spec = whole(ld_shape.shape)
    wide = grid_rows * width
    tile = lanes
    anyspec = pl.BlockSpec(memory_space=pl.ANY)
    stats = (row_stat, own_stat, mate_stat, ld_all)
    stat_specs = [stat_spec] * 3 + [ld_spec]
    held_weights = ()
    span = blocks // 2
    for k in range(2):
        kept = len(held_weights)
        spot = lambda i, _, k=k: (i + k * span, 0, 0)
        held_weights = call(
            functools.partial(weight_kernel, blocks, k * span, kept),
            idx,
            (*stats, *held_weights),
            stat_specs + [anyspec] * kept,
            [
                jax.ShapeDtypeStruct((blocks, 3, width, wide), bf16),
                jax.ShapeDtypeStruct((blocks, snps, width), bf16),
                jax.ShapeDtypeStruct((blocks, snps, wide), bf16),
                jax.ShapeDtypeStruct((blocks, snps, lanes), f32),
            ],
            [
                pl.BlockSpec((None, 3, width, wide), lambda i, _, k=k: (i + k * span, 0, 0, 0)),
                pl.BlockSpec((None, snps, width), spot),
                pl.BlockSpec((None, snps, wide), spot),
                pl.BlockSpec((None, snps, lanes), spot),
            ],
            grid=(span,),
            scratch=[pltpu.VMEM((snps, width), bf16)] * 2,
            flops=6 * span * snps * width * wide,
            aliases={5 + j: j for j in range(kept)},
        )
    w_sums, u_row, u_col, inv_col = held_weights
    outer, last[1], u_row = lax.optimization_barrier((outer, last[1], u_row))
    own = [zscores, near, inner + outer]
    own.append(jnp.concatenate([cross[k] + last[k] for k in range(2)], axis=0))
    mate = mate + [swap(own[slot]) for slot in (2, 3)]
    small = tile
    groups = width // lanes
    out = jax.ShapeDtypeStruct((width * groups * grid_rows, lanes), f32)
    out_spec = pl.BlockSpec((small * groups * grid_rows, lanes), lambda i, _: (jnp.maximum(i - 1, 0), 0))
    return tuple(
        flat.reshape(width, groups, grid_rows, lanes).transpose(0, 2, 1, 3).reshape(1, width, grid_rows, width)
        for flat in call(
            functools.partial(finish_kernel, parts, blocks),
            idx,
            (*first, *rows, *own, *mate, u_row, u_col, inv_col, w_sums, *stats),
            [anyspec] * (2 * parts + 2 * blocks + 4) + stat_specs,
            [out, out],
            [out_spec, out_spec],
            grid=(1 + width // small,),
            scratch=[
                pltpu.VMEM((2, snps, width), bf16),
                pltpu.VMEM((2, snps, width), bf16),
                pltpu.VMEM((2, snps, width), bf16),
                pltpu.VMEM((2, snps, width), bf16),
                pltpu.VMEM((2, snps, wide), bf16),
                pltpu.VMEM((2, snps, lanes), f32),
                pltpu.VMEM((2, snps, width), bf16),
                pltpu.VMEM((2, snps, width), bf16),
                pltpu.VMEM((2, snps, wide), bf16),
                pltpu.VMEM((blocks, 2, width, wide), bf16),
                pltpu.VMEM((blocks, 3, width, wide), bf16),
                pltpu.VMEM((blocks + 1, width, lanes), f32),
                pltpu.VMEM((8, wide), f32),
                pltpu.SemaphoreType.DMA((blocks, 5 + parts)),
                pltpu.SemaphoreType.DMA((1,)),
            ],
            flops=4 * blocks * snps * width * wide,
        )
    )


def general_device(ldscore, zscores):
    blocks = lax.axis_size("genome")
    grid_rows = lax.axis_size("trow")
    grid_cols = lax.axis_size("tcol")
    snp_count = zscores.shape[0]
    shard_width = zscores.shape[1]
    traits = shard_width * grid_rows * grid_cols
    row_width = traits // grid_rows
    row_share = row_width // blocks
    row_index = lax.axis_index("trow")
    col_index = lax.axis_index("tcol")
    genome_index = lax.axis_index("genome")
    ld_weight = 1.0 / ldscore
    z_float = zscores.astype(jnp.float32)
    z_square = z_float * z_float
    own_stats = jnp.stack(
        [jnp.sum(z_square * ld_weight[:, None], axis=0), jnp.sum(z_square, axis=0)]
    )
    own_scalars = jnp.stack([jnp.sum(ld_weight), jnp.sum(ldscore)])
    all_stats, all_scalars = (
        lax.all_gather(own_stats[None], ("genome", "trow", "tcol"), axis=0, tiled=True),
        lax.all_gather(own_scalars[None], ("genome", "trow", "tcol"), axis=0, tiled=True),
    )
    all_stats = all_stats.reshape(blocks, grid_rows * grid_cols, 2, shard_width)
    all_stats = all_stats.transpose(0, 2, 1, 3).reshape(blocks, 2, traits)
    all_scalars = all_scalars.reshape(blocks, grid_rows * grid_cols, 2)[:, 0, :]
    total_stats = jnp.sum(all_stats, axis=0)
    total_scalars = jnp.sum(all_scalars, axis=0)
    herit_full = slope_fit(
        total_scalars[0],
        total_scalars[1],
        total_stats[0],
        total_stats[1],
        float(snp_count * blocks),
    )
    rest_stats = total_stats[None] - all_stats
    rest_scalars = total_scalars[None] - all_scalars
    herit_del = slope_fit(
        rest_scalars[:, 0:1],
        rest_scalars[:, 1:2],
        rest_stats[:, 0],
        rest_stats[:, 1],
        float(snp_count * (blocks - 1)),
    )
    herit_pos = jnp.maximum(herit_full, 0.0)
    col_z = lax.all_gather(zscores, "trow", axis=1, tiled=True)
    col_herit = lax.dynamic_index_in_dim(
        herit_pos.reshape(grid_rows, grid_cols, shard_width), col_index, 1, keepdims=False
    ).reshape(-1)
    col_u = weights_for(col_herit, ldscore)
    col_zu = (col_z.astype(jnp.float32) * col_u.astype(jnp.float32)).astype(jnp.bfloat16)
    piece = lax.all_gather(zscores, "tcol", axis=1, tiled=True)
    herit_rows = lax.dynamic_slice_in_dim(herit_pos, row_index * row_width, piece.shape[1])
    row_u = weights_for(herit_rows, ldscore)
    u_float = row_u.astype(jnp.float32)
    scaled = piece.astype(jnp.float32) * u_float
    row_zu = scaled.astype(jnp.bfloat16)
    row_scaled = (scaled * ld_weight[:, None]).astype(jnp.bfloat16)
    products = [contract(row_scaled, col_zu), contract(row_zu, col_zu)]
    row_inv = (u_float * ld_weight[:, None]).astype(jnp.bfloat16)
    row_ld = (u_float * ldscore[:, None]).astype(jnp.bfloat16)
    products = products + [
        contract(row_inv, col_u),
        contract(row_u, col_u),
        contract(row_ld, col_u),
    ]
    sums = jnp.stack(products)
    sums = sums.astype(jnp.bfloat16)[:, None]
    row_start = row_index * row_width + genome_index * row_share
    tiles = lax.all_to_all(sums, "genome", split_axis=2, concat_axis=1, tiled=True)
    tile_values = tiles.astype(jnp.float32)
    totals = jnp.sum(tile_values, axis=1)
    deleted = totals[:, None] - tile_values
    full_g = coupling(totals)
    del_g = coupling(deleted)
    herit_floor = jnp.maximum(herit_full, floor_value)
    del_floor = jnp.maximum(herit_del, floor_value)
    rows_full = lax.dynamic_slice_in_dim(herit_floor, row_start, row_share)
    cols_full = lax.dynamic_index_in_dim(
        herit_floor.reshape(grid_rows, grid_cols, shard_width), col_index, 1, keepdims=False
    ).reshape(-1)
    rows_del = lax.dynamic_slice_in_dim(del_floor, row_start, row_share, axis=1)
    cols_del = lax.dynamic_index_in_dim(
        del_floor.reshape(blocks, grid_rows, grid_cols, shard_width), col_index, 2, keepdims=False
    ).reshape(blocks, -1)
    rg_tile = full_g / jnp.sqrt(rows_full[:, None] * cols_full[None, :])
    rg_del = del_g / jnp.sqrt(rows_del[:, :, None] * cols_del[:, None, :])
    mean_del = jnp.mean(rg_del, axis=0)
    differ = rg_del - mean_del[None]
    spread = jnp.sum(differ * differ, axis=0)
    se_tile = jnp.sqrt((blocks - 1) / blocks * spread)
    out_shape = (1, row_share, grid_rows, shard_width)
    return (rg_tile.reshape(out_shape), se_tile.reshape(out_shape))


def is_square(sizes):
    return sizes[0] == sizes[2] == 4 and sizes[1] == 2


def solution(mesh):
    sizes = tuple(mesh.shape[name] for name in axes)

    def per_device(ldscore, zscores):
        snps, width = zscores.shape
        if is_square(sizes) and width % lanes == 0 and snps % width == 0 and width // sizes[2] % lanes == 0 and snps % (2 * lanes) == 0:
            return square_device(sizes, ldscore, zscores)
        return general_device(ldscore, zscores)

    step = jax.shard_map(
        per_device,
        mesh=mesh,
        in_specs=(P("genome"), P("genome", ("trow", "tcol"))),
        out_specs=(P("trow", "genome", None, "tcol"), P("trow", "genome", None, "tcol")),
        check_vma=False,
    )
    return step if is_square(sizes) else step
```
